32 devices in a mesh: dp: 4 (over z), row: 4 (over x, core), col: 2 (over y).
Axes of the slice: x: 2, y: 2, z: 4, core: 2. Of those that a mesh axis runs over, the one named last changes fastest.
Arguments:
- hidden: float32 [4096, 1024], P(('dp', 'row')), may hold values from -6 to 6
- cotangent: float32 [4096, 1024], P(('dp', 'row'), 'col'), may hold values from -6 to 6
- norm_gain: float32 [1024], replicated, may hold values from 0.5 to 1.5
- weight_z: bfloat16 [1024, 2048], P('col', 'row'), may hold values from -0.1875 to 0.1875
- weight_x: bfloat16 [1024, 2048], P('col', 'row'), may hold values from -0.1875 to 0.1875
- weight_dt: bfloat16 [1024, 32], P('col', 'row'), may hold values from -0.1875 to 0.1875
- weight_bc: bfloat16 [1024, 256], P('col'), may hold values from -0.1875 to 0.1875
- conv_weight: float32 [4, 2048], P(None, ('row', 'col')), may hold values from -3 to 3
- conv_bias: float32 [2048], P(('row', 'col')), may hold values from -3 to 3
- bc_conv_weight: float32 [4, 256], replicated, may hold values from -3 to 3
- bc_conv_bias: float32 [256], replicated, may hold values from -3 to 3
- dt_bias: float32 [32], P(('row', 'col')), may hold values from -5 to -1
- decay_log: float32 [32], P(('row', 'col')), may hold values from 0 to 2.77
- skip_gain: float32 [32], P(('row', 'col')), may hold values from 0.5 to 1.5
- gate_gain: float32 [2048], P(('row', 'col')), may hold values from 0.25 to 1.75
- out_weight: bfloat16 [2048, 1024], P('row', 'col'), may hold values from -0.125 to 0.125
Outputs:
- output: float32 [4096, 1024], P(('dp', 'row'), 'col')
- grad_hidden: float32 [4096, 1024], P(('dp', 'row'), 'col')
- grad_norm_gain: float32 [1024], P('col')
- grad_weight_z: float32 [1024, 2048], P('col', 'row')
- grad_weight_x: float32 [1024, 2048], P('col', 'row')
- grad_weight_dt: float32 [1024, 32], P('col', 'row')
- grad_weight_bc: float32 [1024, 256], P('col')
- grad_conv_weight: float32 [4, 2048], P(None, ('row', 'col'))
- grad_conv_bias: float32 [2048], P(('row', 'col'))
- grad_bc_conv_weight: float32 [4, 256], replicated
- grad_bc_conv_bias: float32 [256], replicated
- grad_dt_bias: float32 [32], P(('row', 'col'))
- grad_decay_log: float32 [32], P(('row', 'col'))
- grad_skip_gain: float32 [32], P(('row', 'col'))
- grad_gate_gain: float32 [2048], P(('row', 'col'))
- grad_out_weight: float32 [2048, 1024], P('row', 'col')
The draws below stay inside these ranges and needn't reach their ends.
All inputs are finite; a program needn't handle non-finite values.
Results may differ from the reference program's by a relative error of at most 0.012.
Values may be sent and summed in bfloat16 or wider, within the bound.
A program may use at most 128 MiB of HBM per device.

```python
import jax
import jax.numpy as jnp
from jax import lax

D = 1024
HEADS = 32
STATE = 128
KERNEL = 4
BLOCK = 256
SEQ_LEN = 1024
INNER = 2048
TOKENS = 4096


def block_scale(key, extent, cuts, smallest, high):
    factor_of, own = 1.0, jax.random.fold_in(key, 6)
    for position, parts in cuts:
        steps = jnp.exp(jax.random.uniform(jax.random.fold_in(own, position), (parts,), jnp.float32, smallest / len(cuts), high / len(cuts)))
        factor_of = factor_of * jnp.repeat(steps, extent[position] // parts).reshape([-1 if axis == position else 1 for axis in range(len(extent))])
    return factor_of


def scatter_about(stream_key, dims, scale, reach, split=(), kind=jnp.bfloat16):
    drawn = scale * jax.random.normal(stream_key, dims, jnp.float32)
    if split:
        drawn = drawn * block_scale(stream_key, dims, split, -0.22, 0.18)
    return jnp.clip(drawn, -reach, reach).astype(kind)


def setup_inputs(seed: int = 0) -> dict:
    arg_keys = jax.random.split(jax.random.key(seed), 17)
    return {
        "hidden": scatter_about(arg_keys[0], (TOKENS, D), 1.0, 6.0, ((0, 16),), jnp.float32),
        "cotangent": scatter_about(arg_keys[1], (TOKENS, D), 1.0, 6.0, ((0, 16), (1, 2)), jnp.float32),
        "norm_gain": jnp.clip(1.0 + 0.1 * jax.random.normal(arg_keys[2], (D,), jnp.float32), 0.5, 1.5),
        "weight_z": scatter_about(arg_keys[3], (D, INNER), D ** -0.5, 0.1875, ((0, 2), (1, 4))),
        "weight_x": scatter_about(arg_keys[4], (D, INNER), D ** -0.5, 0.1875, ((0, 2), (1, 4))),
        "weight_dt": scatter_about(arg_keys[5], (D, HEADS), D ** -0.5, 0.1875, ((0, 2), (1, 4))),
        "weight_bc": scatter_about(arg_keys[6], (D, 2 * STATE), D ** -0.5, 0.1875, ((0, 2),)),
        "conv_weight": scatter_about(arg_keys[7], (KERNEL, INNER), KERNEL ** -0.5, 3.0, ((1, 8),), jnp.float32),
        "conv_bias": scatter_about(arg_keys[8], (INNER,), 0.5, 3.0, ((0, 8),), jnp.float32),
        "bc_conv_weight": scatter_about(arg_keys[9], (KERNEL, 2 * STATE), KERNEL ** -0.5, 3.0, (), jnp.float32),
        "bc_conv_bias": scatter_about(arg_keys[10], (2 * STATE,), 0.5, 3.0, (), jnp.float32),
        "dt_bias": jnp.clip(-5.0 + 4.0 * jax.random.uniform(arg_keys[11], (HEADS,), jnp.float32) ** block_scale(arg_keys[11], (HEADS,), ((0, 8),), -0.2, 0.2), -5.0, -1.0),
        "decay_log": jnp.clip(2.77 * jax.random.uniform(arg_keys[12], (HEADS,), jnp.float32) ** block_scale(arg_keys[12], (HEADS,), ((0, 8),), -0.2, 0.2), 0.0, 2.77),
        "skip_gain": jnp.clip(0.5 + 1.0 * jax.random.uniform(arg_keys[13], (HEADS,), jnp.float32) ** block_scale(arg_keys[13], (HEADS,), ((0, 8),), -0.2, 0.2), 0.5, 1.5),
        "gate_gain": jnp.clip(1.0 + 0.15 * jax.random.normal(arg_keys[14], (INNER,), jnp.float32), 0.25, 1.75),
        "out_weight": scatter_about(arg_keys[15], (INNER, D), INNER ** -0.5, 0.125, ((0, 4), (1, 2))),
    }


EPSILON = 1e-05
PRECISE = lax.Precision.HIGHEST

def causal_conv(values, kernel, offset_bias):
    kernel_width = kernel.shape[0]
    length = values.shape[0]
    padded = jnp.pad(values, ((kernel_width - 1, 0), (0, 0)))
    summed = jnp.broadcast_to(offset_bias[None, :], values.shape)
    for offset in range(kernel_width):
        summed = summed + kernel[offset][None, :] * padded[offset:offset + length]
    return summed

def block_scan(inputs, step_sizes, rates, b_values, c_values):
    length, head_count, head_width = inputs.shape
    block_count = length // BLOCK
    state_width = b_values.shape[1]
    blocks = inputs.reshape(block_count, BLOCK, head_count, head_width)
    block_steps = step_sizes.reshape(block_count, BLOCK, head_count)
    log_decay = jnp.cumsum(block_steps * rates[None, None, :], axis=1)
    b_blocks = b_values.reshape(block_count, BLOCK, state_width)
    c_blocks = c_values.reshape(block_count, BLOCK, state_width)
    scores = jnp.einsum('cln,csn->cls', c_blocks, b_blocks, precision=PRECISE)
    causal = jnp.arange(BLOCK)[:, None] >= jnp.arange(BLOCK)[None, :]
    log_gap = log_decay[:, :, None, :] - log_decay[:, None, :, :]
    decays = jnp.exp(jnp.where(causal[None, :, :, None], log_gap, -1e+30))
    mixing = scores[:, :, :, None] * decays * block_steps[:, None, :, :]
    inside = jnp.einsum('clsh,cshp->clhp', mixing, blocks, precision=PRECISE)
    tail_decay = jnp.exp(log_decay[:, -1:, :] - log_decay) * block_steps
    states = jnp.einsum('csn,csh,cshp->chpn', b_blocks, tail_decay, blocks, precision=PRECISE)
    carried = jnp.exp(log_decay[:, -1, :])

    def advance(running, pair_item):
        new_state, factor = pair_item
        return (running * factor[:, None, None] + new_state, running)
    initial = jnp.zeros((head_count, head_width, state_width), jnp.float32)
    _, entering = lax.scan(advance, initial, (states, carried))
    outside = jnp.einsum('cln,chpn,clh->clhp', c_blocks, entering, jnp.exp(log_decay), precision=PRECISE)
    return (inside + outside).reshape(length, head_count, head_width)

def sequence_mixer(z_raw, x_raw, step_raw, bc_raw, conv_weight, conv_bias, bc_conv_weight, bc_conv_bias, dt_bias, decay_log, skip_gain):
    x_conv = jax.nn.silu(causal_conv(x_raw, conv_weight, conv_bias))
    bc_conv = jax.nn.silu(causal_conv(bc_raw, bc_conv_weight, bc_conv_bias))
    state_width = bc_conv.shape[1] // 2
    head_count = step_raw.shape[1]
    length = x_conv.shape[0]
    heads_in = x_conv.reshape(length, head_count, -1)
    step_size = jax.nn.softplus(step_raw + dt_bias[None, :])
    rates = -jnp.exp(decay_log)
    mixed = block_scan(heads_in, step_size, rates, bc_conv[:, :state_width], bc_conv[:, state_width:])
    mixed = mixed + skip_gain[None, :, None] * heads_in
    return mixed.reshape(length, -1) * jax.nn.silu(z_raw)

def reference(hidden, cotangent, norm_gain, weight_z, weight_x, weight_dt, weight_bc, conv_weight, conv_bias, bc_conv_weight, bc_conv_bias, dt_bias, decay_log, skip_gain, gate_gain, out_weight):
    seq_count = hidden.shape[0] // SEQ_LEN
    model_width = hidden.shape[1]
    hidden_seqs = hidden.reshape(seq_count, SEQ_LEN, model_width)
    cot_seqs = cotangent.reshape(seq_count, SEQ_LEN, model_width)
    bc_wide = weight_bc.astype(jnp.float32)

    def one_sequence(totals, pair_item):
        seq_rows, seq_cot = pair_item
        inv_rms = lax.rsqrt(lax.optimization_barrier(jnp.mean(seq_rows * seq_rows, axis=1, keepdims=True)) + EPSILON)
        normed = seq_rows * inv_rms
        scaled = (normed * norm_gain[None, :]).astype(jnp.bfloat16)
        z_raw = jnp.dot(scaled, weight_z, preferred_element_type=jnp.float32)
        x_raw = jnp.dot(scaled, weight_x, preferred_element_type=jnp.float32)
        step_raw = jnp.dot(scaled, weight_dt, preferred_element_type=jnp.float32)
        bc_raw = jnp.dot(scaled, weight_bc, preferred_element_type=jnp.float32)
        gated, pullback = jax.vjp(sequence_mixer, z_raw, x_raw, step_raw, bc_raw, conv_weight, conv_bias, bc_conv_weight, bc_conv_bias, dt_bias, decay_log, skip_gain)
        inv_gate = lax.rsqrt(lax.optimization_barrier(jnp.mean(gated * gated, axis=1, keepdims=True)) + EPSILON)
        gate_hat = gated * inv_gate
        gate_out = (gate_hat * gate_gain[None, :]).astype(jnp.bfloat16)
        seq_out = seq_rows + jnp.dot(gate_out, out_weight, preferred_element_type=jnp.float32)
        cot_half = seq_cot.astype(jnp.bfloat16)
        grad_out_weight = jnp.dot(gate_out.T, cot_half, preferred_element_type=jnp.float32)
        grad_gate_out = jnp.dot(cot_half, out_weight.T, preferred_element_type=jnp.float32)
        grad_gate_gain = lax.optimization_barrier(jnp.sum(grad_gate_out * gate_hat, axis=0))
        grad_hat = grad_gate_out * gate_gain[None, :]
        grad_gated = inv_gate * (grad_hat - gate_hat * lax.optimization_barrier(jnp.mean(grad_hat * gate_hat, axis=1, keepdims=True)))
        grads = pullback(grad_gated)
        grad_bc = grads[3]
        z_half = grads[0].astype(jnp.bfloat16)
        x_half = grads[1].astype(jnp.bfloat16)
        step_half = grads[2].astype(jnp.bfloat16)
        grad_scaled = jnp.dot(z_half, weight_z.T, preferred_element_type=jnp.float32)
        grad_scaled = grad_scaled + jnp.dot(x_half, weight_x.T, preferred_element_type=jnp.float32)
        grad_scaled = grad_scaled + jnp.dot(step_half, weight_dt.T, preferred_element_type=jnp.float32)
        grad_scaled = grad_scaled + jnp.dot(grad_bc, bc_wide.T, precision=PRECISE)
        seq_grads = (lax.optimization_barrier(jnp.sum(grad_scaled * normed, axis=0)), jnp.dot(scaled.T, z_half, preferred_element_type=jnp.float32), jnp.dot(scaled.T, x_half, preferred_element_type=jnp.float32), jnp.dot(scaled.T, step_half, preferred_element_type=jnp.float32), jnp.dot(scaled.astype(jnp.float32).T, grad_bc, precision=PRECISE), grads[4], grads[5], grads[6], grads[7], grads[8], grads[9], grads[10], grad_gate_gain, grad_out_weight)
        grad_in = grad_scaled * norm_gain[None, :]
        seq_grad_hidden = seq_cot + inv_rms * (grad_in - normed * lax.optimization_barrier(jnp.mean(grad_in * normed, axis=1, keepdims=True)))
        return (jax.tree.map(jnp.add, totals, seq_grads), (seq_out, seq_grad_hidden))
    initial = tuple((jnp.zeros(item.shape, jnp.float32) for item in (norm_gain, weight_z, weight_x, weight_dt, weight_bc, conv_weight, conv_bias, bc_conv_weight, bc_conv_bias, dt_bias, decay_log, skip_gain, gate_gain, out_weight)))
    totals, (outputs, grad_rows) = lax.scan(one_sequence, initial, (hidden_seqs, cot_seqs))
    output = outputs.reshape(hidden.shape)
    grad_hidden = grad_rows.reshape(hidden.shape)
    return (output, grad_hidden, totals[0], totals[1], totals[2], totals[3], totals[4], totals[5], totals[6], totals[7], totals[8], totals[9], totals[10], totals[11], totals[12], totals[13])
```

```python
import functools

import jax
import jax.numpy as jnp
from jax import lax
from jax.experimental import pallas as pl
from jax.experimental.pallas import tpu as pltpu
from jax.sharding import PartitionSpec as P

BLOCK = 256
SEQ_LEN = 1024
LANES = 128
HALO = 8
EPSILON = 1e-05
PRECISE = lax.Precision.HIGHEST
F32 = jnp.float32
BF16 = jnp.bfloat16


def dot_f32(a, b):
    return jnp.dot(a, b, precision=PRECISE, preferred_element_type=F32)


def dot_nn(a, b):
    return lax.dot_general(a, b, (((1,), (0,)), ((), ())), preferred_element_type=F32)


def dot_nt(a, b):
    return lax.dot_general(a, b, (((1,), (1,)), ((), ())), preferred_element_type=F32)


def dot_tn(a, b):
    return lax.dot_general(a, b, (((0,), (0,)), ((), ())), preferred_element_type=F32)


def sigmoid(v):
    return 1.0 / (1.0 + jnp.exp(-v))


def iota(shape, axis):
    return lax.broadcasted_iota(jnp.int32, shape, axis)


def head_spread(chan, head_width):
    head = iota((LANES, chan), 0)
    lane = iota((LANES, chan), 1)
    return ((lane >= head * head_width) & (lane < (head + 1) * head_width)).astype(F32)


def block_terms(ext_ref, step_raw, conv_ref, head_ref, chan, head_width):
    rows = step_raw.shape[0]
    pre = conv_ref[4:5, :]
    for tap in range(4):
        first = HALO - 3 + tap
        pre = pre + conv_ref[tap : tap + 1, :] * ext_ref[first : first + rows, :]
    gate = sigmoid(pre)
    conv = pre * gate
    step_pre = step_raw + head_ref[0:1, :]
    step = jnp.maximum(step_pre, 0.0) + jnp.log1p(jnp.exp(-jnp.abs(step_pre)))
    rate = -jnp.exp(head_ref[1:2, :])
    causal = iota((rows, rows), 0) >= iota((rows, rows), 1)
    log_decay = dot_f32(causal.astype(F32), step * rate)
    spread = head_spread(chan, head_width)
    step_ch = dot_f32(step, spread)
    log_ch = dot_f32(log_decay, spread)
    skip_ch = dot_f32(jnp.broadcast_to(head_ref[2:3, :], (HALO, LANES)), spread)[0:1, :]
    return pre, gate, conv, step_pre, step, rate, causal, log_decay, spread, step_ch, log_ch, skip_ch


def forward_kernel(heads, head_width, proj_ref, conv_ref, head_ref, gated_ref, mixed_ref, inside_ref, state_ref, ext, state):
    chan = heads * head_width
    rows = proj_ref.shape[0]
    wide = ext.shape[1]

    @pl.when(pl.program_id(0) == 0)
    def _():
        ext[...] = jnp.zeros_like(ext)
        state[...] = jnp.zeros_like(state)

    ext[0:HALO, :] = ext[rows : rows + HALO, :]
    ext[HALO : HALO + rows, :] = proj_ref[:, chan : chan + wide]
    z_raw = proj_ref[:, 0:chan]
    terms = block_terms(ext, proj_ref[:, chan + wide :], conv_ref, head_ref, chan, head_width)
    _, _, conv, _, step, _, causal, log_decay, _, step_ch, log_ch, skip_ch = terms
    half = (wide - chan) // 2
    x_conv = conv[:, :chan]
    b_half = conv[:, chan : chan + half].astype(BF16)
    c_half = conv[:, chan + half :].astype(BF16)
    stepped = x_conv * step_ch
    stepped_half = stepped.astype(BF16)
    scores = dot_nt(c_half, b_half)
    log_rows = log_decay.T
    lane = iota((rows, chan), 1)
    inside = jnp.zeros((rows, chan), F32)
    for head in range(heads):
        gap = log_decay[:, head : head + 1] - log_rows[head : head + 1, :]
        mixing = (scores * jnp.exp(jnp.where(causal, gap, -1e30))).astype(BF16)
        mine = (lane >= head * head_width) & (lane < (head + 1) * head_width)
        inside = inside + dot_nn(mixing, jnp.where(mine, stepped, 0.0).astype(BF16))
    entering = state[...]
    state_ref[0] = entering
    outside = dot_nn(c_half, entering.astype(BF16)) * jnp.exp(log_ch)
    mixed = inside + outside + skip_ch * x_conv
    last = log_ch[rows - 1 : rows, :]
    tail = stepped * jnp.exp(last - log_ch)
    state[...] = entering * jnp.exp(last) + dot_tn(b_half, tail.astype(BF16))
    gated_ref[...] = mixed * (z_raw * sigmoid(z_raw))
    mixed_ref[...] = mixed
    inside_ref[...] = inside


def backward_kernel(
    heads, head_width, proj_ref, prior_ref, conv_ref, head_ref, mixed_ref, inside_ref, state_ref, grad_ref,
    slot_ref, conv_grad_ref, head_grad_ref, skip_grad_ref, ext, grad_ext, grad_state,
):
    chan = heads * head_width
    rows = proj_ref.shape[0]
    wide = ext.shape[1]
    turn = pl.program_id(0)
    first_block = turn == pl.num_programs(0) - 1

    @pl.when(turn == 0)
    def _():
        grad_ext[...] = jnp.zeros_like(grad_ext)
        grad_state[...] = jnp.zeros_like(grad_state)
        conv_grad_ref[...] = jnp.zeros_like(conv_grad_ref)
        head_grad_ref[...] = jnp.zeros_like(head_grad_ref)
        skip_grad_ref[...] = jnp.zeros_like(skip_grad_ref)

    ext[0:HALO, :] = jnp.where(first_block, 0.0, prior_ref[:, chan : chan + wide])
    ext[HALO : HALO + rows, :] = proj_ref[:, chan : chan + wide]
    terms = block_terms(ext, proj_ref[:, chan + wide :], conv_ref, head_ref, chan, head_width)
    pre, gate, conv, step_pre, step, rate, causal, log_decay, spread, step_ch, log_ch, skip_ch = terms
    half = (wide - chan) // 2
    x_conv = conv[:, :chan]
    b_half = conv[:, chan : chan + half].astype(BF16)
    c_half = conv[:, chan + half :].astype(BF16)
    stepped = x_conv * step_ch
    stepped_half = stepped.astype(BF16)
    grad_mixed = grad_ref[...]
    grad_half = grad_mixed.astype(BF16)
    inside = inside_ref[...]
    outside = mixed_ref[...] - inside - skip_ch * x_conv

    scores = dot_nt(c_half, b_half)
    log_rows = log_decay.T
    lane = iota((rows, chan), 1)
    grad_scores = jnp.zeros((rows, rows), F32)
    grad_inner = jnp.zeros((rows, chan), F32)
    for head in range(heads):
        gap = log_decay[:, head : head + 1] - log_rows[head : head + 1, :]
        decay = jnp.exp(jnp.where(causal, gap, -1e30))
        mixing = (scores * decay).astype(BF16)
        mine = (lane >= head * head_width) & (lane < (head + 1) * head_width)
        grad_mine = jnp.where(mine, grad_mixed, 0.0).astype(BF16)
        grad_scores = grad_scores + dot_nt(grad_mine, stepped_half) * decay
        grad_inner = grad_inner + dot_tn(mixing, grad_mine)
    scores_half = grad_scores.astype(BF16)

    entering = state_ref[0]
    left = grad_state[...]
    left_half = left.astype(BF16)
    grad_outer = (grad_mixed * jnp.exp(log_ch)).astype(BF16)
    last = log_ch[rows - 1 : rows, :]
    fade = jnp.exp(last - log_ch)
    tail = stepped * fade
    grad_tail = dot_nn(b_half, left_half)
    tail_term = tail * grad_tail
    grad_c = dot_nt(grad_outer, entering.astype(BF16)) + dot_nn(scores_half, b_half)
    grad_b = dot_nt(tail.astype(BF16), left_half) + dot_tn(scores_half, c_half)
    grad_last = jnp.sum(tail_term, axis=0, keepdims=True) + jnp.exp(last) * jnp.sum(
        left * entering, axis=0, keepdims=True
    )
    grad_state[...] = left * jnp.exp(last) + dot_tn(c_half, grad_outer)

    grad_stepped = grad_inner + grad_tail * fade
    log_term = (
        grad_half.astype(F32) * inside
        + grad_mixed * outside
        - stepped_half.astype(F32) * grad_inner
        - tail_term
    )
    row = iota((rows, chan), 0)
    log_term = log_term + jnp.where(row == rows - 1, grad_last, 0.0)

    def per_head(values):
        return lax.dot_general(
            values, spread, (((1,), (1,)), ((), ())), precision=PRECISE, preferred_element_type=F32
        )

    later = (iota((rows, rows), 0) <= iota((rows, rows), 1)).astype(F32)
    grad_rate_step = dot_f32(later, per_head(log_term))
    grad_step = per_head(grad_stepped * x_conv) + grad_rate_step * rate
    grad_step_raw = grad_step * sigmoid(step_pre)
    head_grad_ref[0:1, :] += jnp.sum(grad_step_raw, axis=0, keepdims=True)
    head_grad_ref[1:2, :] += jnp.sum(grad_rate_step * step, axis=0, keepdims=True) * rate
    skip_grad_ref[0:1, :] += jnp.sum(grad_mixed * x_conv, axis=0, keepdims=True)

    grad_x = grad_stepped * step_ch + grad_mixed * skip_ch
    slope = gate * (1.0 + pre * (1.0 - gate))
    grad_ext[rows : rows + HALO, :] = grad_ext[0:HALO, :]
    grad_ext[0:rows, 0:chan] = grad_x * slope[:, :chan]
    grad_ext[0:rows, chan : chan + half] = grad_b * slope[:, chan : chan + half]
    grad_ext[0:rows, chan + half :] = grad_c * slope[:, chan + half :]
    grad_pre = grad_ext[0:rows, :]
    grad_raw = jnp.zeros((rows, wide), F32)
    for tap in range(4):
        grad_raw = grad_raw + conv_ref[tap : tap + 1, :] * grad_ext[3 - tap : 3 - tap + rows, :]
        first = HALO - 3 + tap
        conv_grad_ref[tap : tap + 1, :] += jnp.sum(
            grad_pre * ext[first : first + rows, :], axis=0, keepdims=True
        )
    conv_grad_ref[4:5, :] += jnp.sum(grad_pre, axis=0, keepdims=True)
    slot_ref[:, 0:wide] = grad_raw.astype(BF16)
    slot_ref[:, wide:] = grad_step_raw.astype(BF16)


def mixer_forward(proj, conv_pack, head_pack, heads, head_width, wide):
    total, columns = proj.shape
    chan = heads * head_width
    state_width = (wide - chan) // 2
    blocks = total // BLOCK
    row_spec = pl.BlockSpec((BLOCK, chan), lambda i: (i, 0))
    rows = jax.ShapeDtypeStruct((total, chan), F32)
    return pl.pallas_call(
        functools.partial(forward_kernel, heads, head_width),
        grid=(blocks,),
        in_specs=[
            pl.BlockSpec((BLOCK, columns), lambda i: (i, 0)),
            pl.BlockSpec(conv_pack.shape, lambda i: (0, 0)),
            pl.BlockSpec(head_pack.shape, lambda i: (0, 0)),
        ],
        out_specs=[row_spec, row_spec, row_spec, pl.BlockSpec((1, state_width, chan), lambda i: (i, 0, 0))],
        out_shape=[rows, rows, rows, jax.ShapeDtypeStruct((blocks, state_width, chan), F32)],
        scratch_shapes=[pltpu.VMEM((BLOCK + HALO, wide), F32), pltpu.VMEM((state_width, chan), F32)],
        compiler_params=pltpu.CompilerParams(vmem_limit_bytes=32 << 20),
        cost_estimate=pl.CostEstimate(flops=4 * 10**9, bytes_accessed=7 << 20, transcendentals=2 << 20),
        name="mixer_forward",
    )(proj, conv_pack, head_pack)


def mixer_backward(proj, conv_pack, head_pack, mixed, inside, states, grad_mixed, heads, head_width, wide):
    total, columns = proj.shape
    chan = heads * head_width
    state_width = (wide - chan) // 2
    blocks = total // BLOCK
    ratio = BLOCK // HALO
    back = lambda i: (blocks - 1 - i, 0)
    row_spec = pl.BlockSpec((BLOCK, chan), back)
    fixed = lambda i: (0, 0)
    out_columns = wide + LANES
    return pl.pallas_call(
        functools.partial(backward_kernel, heads, head_width),
        grid=(blocks,),
        in_specs=[
            pl.BlockSpec((BLOCK, columns), back),
            pl.BlockSpec((HALO, columns), lambda i: (jnp.maximum((blocks - 1 - i) * ratio - 1, 0), 0)),
            pl.BlockSpec(conv_pack.shape, fixed),
            pl.BlockSpec(head_pack.shape, fixed),
            row_spec,
            row_spec,
            pl.BlockSpec((1, state_width, chan), lambda i: (blocks - 1 - i, 0, 0)),
            row_spec,
        ],
        out_specs=[
            pl.BlockSpec((BLOCK, out_columns), back),
            pl.BlockSpec((HALO, wide), fixed),
            pl.BlockSpec((HALO, LANES), fixed),
            pl.BlockSpec((HALO, chan), fixed),
        ],
        out_shape=[
            jax.ShapeDtypeStruct((total, out_columns), BF16),
            jax.ShapeDtypeStruct((HALO, wide), F32),
            jax.ShapeDtypeStruct((HALO, LANES), F32),
            jax.ShapeDtypeStruct((HALO, chan), F32),
        ],
        scratch_shapes=[
            pltpu.VMEM((BLOCK + HALO, wide), F32),
            pltpu.VMEM((BLOCK + HALO, wide), F32),
            pltpu.VMEM((state_width, chan), F32),
        ],
        compiler_params=pltpu.CompilerParams(vmem_limit_bytes=40 << 20),
        cost_estimate=pl.CostEstimate(flops=12 * 10**9, bytes_accessed=9 << 20, transcendentals=2 << 20),
        name="mixer_backward",
    )(proj, proj, conv_pack, head_pack, mixed, inside, states, grad_mixed)


def from_columns(block_for):
    count = lax.axis_size("col")
    got = [block_for(0)]
    for j in range(1, count):
        pairs = [((i + j) % count, i) for i in range(count)]
        got.append(lax.ppermute(block_for((count - j) % count), "col", pairs))
    return got


def scatter_sum(partial):
    rows, cols = lax.axis_size("row"), lax.axis_size("col")
    pair = 2 if rows % 2 == 0 else 1
    chips = rows // pair
    row = lax.axis_index("row")
    chip, core = row // pair, row % pair
    tokens, width = partial.shape[0] // rows, partial.shape[1] // cols
    blocks = partial.reshape(chips, pair, tokens, cols * width)
    keep = lax.dynamic_index_in_dim(blocks, core, 1, keepdims=False)
    if pair == 2:
        send = lax.dynamic_index_in_dim(blocks, 1 - core, 1, keepdims=False).astype(BF16)
        swap = [(i, i ^ 1) for i in range(rows)]
        keep = keep + lax.ppermute(send, "row", swap).astype(F32)
    total = None
    for dx in range(chips):
        mine = lax.dynamic_index_in_dim(keep, (chip + dx) % chips, 0, keepdims=False)
        for dc in range(cols):
            piece = mine[:, dc * width : (dc + 1) * width]
            if dx or dc:
                pairs = []
                for r in range(rows):
                    for c in range(cols):
                        there = ((r // pair + dx) % chips) * pair + r % pair
                        pairs.append((r * cols + c, there * cols + (c + dc) % cols))
                piece = lax.ppermute(piece.astype(BF16), ("row", "col"), pairs).astype(F32)
            total = piece if total is None else total + piece
    return total


def pad_to(matrix, rows, columns):
    return jnp.pad(matrix, ((0, rows - matrix.shape[0]), (0, columns - matrix.shape[1])))


def body(
    hidden,
    cotangent,
    norm_gain,
    weight_z,
    weight_x,
    weight_dt,
    weight_bc,
    conv_weight,
    conv_bias,
    bc_conv_weight,
    bc_conv_bias,
    dt_bias,
    decay_log,
    skip_gain,
    gate_gain,
    out_weight,
):
    row_count = lax.axis_size("row")
    col_count = lax.axis_size("col")
    col_index = lax.axis_index("col")
    model_width = hidden.shape[1]
    width = weight_z.shape[0]
    chan = weight_z.shape[1] // col_count
    heads = weight_dt.shape[1] // col_count
    head_width = chan // heads
    bc_width = weight_bc.shape[1]
    wide = chan + bc_width
    inner = chan * row_count * col_count

    def own_first(matrix, axis):
        return jnp.roll(matrix, -col_index * width, axis)

    def by_col(matrix, k):
        split = matrix.reshape(matrix.shape[0], col_count, matrix.shape[1] // col_count)
        return lax.dynamic_index_in_dim(split, (col_index + k) % col_count, 1, keepdims=False)

    def weights_for(k):
        return jnp.concatenate(
            [by_col(weight_z, k), by_col(weight_x, k), weight_bc, by_col(weight_dt, k)], axis=1
        )

    weights = jnp.concatenate(from_columns(weights_for), axis=0)
    weights = jnp.pad(weights, ((0, 0), (0, LANES - heads)))

    def out_rows_for(k):
        split = out_weight.reshape(col_count, chan, out_weight.shape[1])
        return lax.dynamic_index_in_dim(split, (col_index + k) % col_count, 0, keepdims=False)

    out_own = jnp.concatenate(from_columns(out_rows_for), axis=1)
    cot_half = cotangent.astype(BF16)
    cot_wide = jnp.concatenate(from_columns(lambda k: cot_half), axis=1)

    inv_rms = lax.rsqrt(jnp.mean(hidden * hidden, axis=1, keepdims=True) + EPSILON)
    scaled = (own_first(hidden, 1) * inv_rms * own_first(norm_gain, 0)[None, :]).astype(BF16)
    gathered = lax.all_gather(scaled, "row", axis=0, tiled=True)
    cot_rows = lax.all_gather(cot_wide, "row", axis=0, tiled=True)
    proj = jnp.dot(gathered, weights, preferred_element_type=F32)

    conv_pack = pad_to(
        jnp.concatenate(
            [
                jnp.concatenate([conv_weight, bc_conv_weight], axis=1),
                jnp.concatenate([conv_bias, bc_conv_bias])[None, :],
            ],
            axis=0,
        ),
        HALO,
        wide,
    )
    head_pack = pad_to(jnp.stack([dt_bias, decay_log, skip_gain]), HALO, LANES)
    gated, mixed, inside, states = mixer_forward(proj, conv_pack, head_pack, heads, head_width, wide)

    grad_gate_out = dot_nt(cot_rows, out_own)
    grad_hat = grad_gate_out * gate_gain[None, :]
    sums = lax.psum(
        jnp.stack([jnp.sum(gated * gated, axis=1), jnp.sum(grad_hat * gated, axis=1)]), ("row", "col")
    )
    inv_gate = lax.rsqrt(sums[0] / inner + EPSILON)[:, None]
    gate_dot = sums[1][:, None] * inv_gate
    gate_hat = gated * inv_gate
    grad_gated = inv_gate * (grad_hat - gate_hat * (gate_dot / inner))
    z_raw = proj[:, :chan]
    z_gate = sigmoid(z_raw)
    grad_mixed = grad_gated * (z_raw * z_gate)
    grad_z = (grad_gated * mixed * (z_gate * (1.0 + z_raw * (1.0 - z_gate)))).astype(BF16)
    gate_out = (gate_hat * gate_gain[None, :]).astype(BF16)
    grad_gate_gain = jnp.sum(grad_gate_out * gate_hat, axis=0)

    slots, conv_grads, head_grads, skip_grads = mixer_backward(
        proj, conv_pack, head_pack, mixed, inside, states, grad_mixed, heads, head_width, wide
    )

    def to_col_blocks(matrix):
        return matrix.reshape(col_count, matrix.shape[0] // col_count, matrix.shape[1])

    def in_col_order(relative, axis):
        return jnp.roll(relative, col_index, axis)

    out_part = dot_tn(gate_out, cot_rows)
    out_rel = from_columns(lambda k: out_part[:, k * width : (k + 1) * width].astype(BF16))
    z_part = dot_tn(gathered, grad_z)
    z_blocks = to_col_blocks(z_part)
    z_rel = from_columns(lambda k: z_blocks[k].astype(BF16))
    early = lax.psum(jnp.concatenate([piece.reshape(-1, chan) for piece in out_rel + z_rel], axis=0), "dp")
    out_size = chan * width // chan
    out_sum = early[: out_size * col_count].reshape(col_count, chan, width)
    z_sum = early[out_size * col_count :].reshape(col_count, width, chan)
    grad_out_weight = in_col_order(out_sum, 0).reshape(col_count * chan, width).astype(F32)
    grad_weight_z = (
        in_col_order(z_sum, 0).transpose(1, 0, 2).reshape(width, col_count * chan).astype(F32)
    )

    branch_out = scatter_sum(dot_nn(gate_out, out_own))
    hidden_col = lax.dynamic_slice_in_dim(hidden, col_index * width, width, 1)
    output = hidden_col + branch_out

    grad_slots = jnp.concatenate([grad_z, slots], axis=1)
    grad_scaled = scatter_sum(dot_nt(grad_slots, weights))

    late_part = dot_tn(gathered, slots)
    weights_f32 = weights.astype(F32)
    gain_part = jnp.sum(z_part * weights_f32[:, :chan], axis=1) + jnp.sum(
        late_part * weights_f32[:, chan:], axis=1
    )
    late_blocks = to_col_blocks(late_part[:, : wide + heads])
    gain_blocks = gain_part.reshape(col_count, 1, width)
    bc_rows = conv_grads[:5, chan:]

    def late_for(k):
        return late_blocks[k].astype(BF16)

    def small_for(k):
        return jnp.concatenate([pad_to(bc_rows, 5, width), gain_blocks[k]], axis=0)

    late_rel = from_columns(late_for)
    small_rel = from_columns(small_for)
    x_rows = [piece[:, :chan] for piece in late_rel]
    dt_rows = [piece[:, wide:].reshape(-1, chan) for piece in late_rel]
    skip_sum = jnp.sum(skip_grads[0].reshape(heads, head_width), axis=1)
    head_row = jnp.concatenate([head_grads[0, :heads], head_grads[1, :heads], skip_sum])[None, :]
    dp_rows = x_rows + dt_rows + [
        conv_grads[:5, :chan].astype(BF16),
        grad_gate_gain[None, :].astype(BF16),
        pad_to(head_row, 1, chan).astype(BF16),
    ]
    late = lax.psum(jnp.concatenate(dp_rows, axis=0), "dp")
    bc_mine = sum(piece[:, chan:wide].astype(F32) for piece in late_rel).astype(BF16)
    small_mine = sum(small_rel)
    shared = lax.psum(
        jnp.concatenate(
            [bc_mine, small_mine[:5, :bc_width].astype(BF16), small_mine[5].reshape(-1, bc_width).astype(BF16)],
            axis=0,
        ),
        ("dp", "row"),
    ).astype(F32)

    dt_count = width * heads // chan
    x_sum = late[: width * col_count].reshape(col_count, width, chan)
    grad_weight_x = (
        in_col_order(x_sum, 0).transpose(1, 0, 2).reshape(width, col_count * chan).astype(F32)
    )
    at = width * col_count
    dt_sum = late[at : at + dt_count * col_count].reshape(col_count, width, heads)
    grad_weight_dt = (
        in_col_order(dt_sum, 0).transpose(1, 0, 2).reshape(width, col_count * heads).astype(F32)
    )
    rest = late[at + dt_count * col_count :].astype(F32)
    grad_weight_bc = shared[:width]
    gain_col = lax.dynamic_slice_in_dim(norm_gain, col_index * width, width, 0)
    grad_norm_gain = shared[width + 5 :].reshape(-1) / gain_col

    normed_col = hidden_col * inv_rms
    grad_in = grad_scaled * gain_col[None, :]
    input_dot = sum(from_columns(lambda k: jnp.sum(grad_in * normed_col, axis=1)))
    grad_hidden = cotangent + inv_rms * (grad_in - normed_col * (input_dot[:, None] / model_width))
    return (
        output,
        grad_hidden,
        grad_norm_gain,
        grad_weight_z,
        grad_weight_x,
        grad_weight_dt,
        grad_weight_bc,
        rest[0:4],
        rest[4],
        shared[width : width + 4],
        shared[width + 4],
        rest[6, :heads],
        rest[6, heads : 2 * heads],
        rest[6, 2 * heads : 3 * heads],
        rest[5],
        grad_out_weight,
    )


def solution(mesh):
    in_specs = (
        P(("dp", "row"), None),
        P(("dp", "row"), "col"),
        P(),
        P("col", "row"),
        P("col", "row"),
        P("col", "row"),
        P("col", None),
        P(None, ("row", "col")),
        P(("row", "col")),
        P(),
        P(),
        P(("row", "col")),
        P(("row", "col")),
        P(("row", "col")),
        P(("row", "col")),
        P("row", "col"),
    )
    out_specs = (
        P(("dp", "row"), "col"),
        P(("dp", "row"), "col"),
        P("col"),
        P("col", "row"),
        P("col", "row"),
        P("col", "row"),
        P("col", None),
        P(None, ("row", "col")),
        P(("row", "col")),
        P(),
        P(),
        P(("row", "col")),
        P(("row", "col")),
        P(("row", "col")),
        P(("row", "col")),
        P("row", "col"),
    )
    return jax.shard_map(body, mesh=mesh, in_specs=in_specs, out_specs=out_specs, check_vma=False)
```

```python
import functools

import jax
import jax.numpy as jnp
from jax import lax
from jax.experimental import pallas as pl
from jax.experimental.pallas import tpu as pltpu
from jax.sharding import PartitionSpec as P

BLOCK = 256
SEQ_LEN = 1024
LANES = 128
HALO = 8
EPSILON = 1e-05
PRECISE = lax.Precision.HIGHEST
F32 = jnp.float32
BF16 = jnp.bfloat16


def dot_f32(a, b):
    return jnp.dot(a, b, precision=PRECISE, preferred_element_type=F32)


def dot_nn(a, b):
    return lax.dot_general(a, b, (((1,), (0,)), ((), ())), preferred_element_type=F32)


def dot_nt(a, b):
    return lax.dot_general(a, b, (((1,), (1,)), ((), ())), preferred_element_type=F32)


def dot_tn(a, b):
    return lax.dot_general(a, b, (((0,), (0,)), ((), ())), preferred_element_type=F32)


def sigmoid(v):
    return 1.0 / (1.0 + jnp.exp(-v))


def iota(shape, axis):
    return lax.broadcasted_iota(jnp.int32, shape, axis)


def head_spread(chan, head_width):
    head = iota((LANES, chan), 0)
    lane = iota((LANES, chan), 1)
    return ((lane >= head * head_width) & (lane < (head + 1) * head_width)).astype(F32)


def block_terms(ext_ref, step_raw, conv_ref, head_ref, chan, head_width):
    rows = step_raw.shape[0]
    pre = conv_ref[4:5, :]
    for tap in range(4):
        first = HALO - 3 + tap
        pre = pre + conv_ref[tap : tap + 1, :] * ext_ref[first : first + rows, :]
    gate = sigmoid(pre)
    conv = pre * gate
    step_pre = step_raw + head_ref[0:1, :]
    step = jnp.maximum(step_pre, 0.0) + jnp.log1p(jnp.exp(-jnp.abs(step_pre)))
    rate = -jnp.exp(head_ref[1:2, :])
    causal = iota((rows, rows), 0) >= iota((rows, rows), 1)
    log_decay = dot_f32(causal.astype(F32), step * rate)
    spread = head_spread(chan, head_width)
    step_ch = dot_f32(step, spread)
    log_ch = dot_f32(log_decay, spread)
    skip_ch = dot_f32(jnp.broadcast_to(head_ref[2:3, :], (HALO, LANES)), spread)[0:1, :]
    return pre, gate, conv, step_pre, step, rate, causal, log_decay, spread, step_ch, log_ch, skip_ch


def forward_kernel(heads, head_width, proj_ref, conv_ref, head_ref, gated_ref, mixed_ref, inside_ref, state_ref, ext, state):
    chan = heads * head_width
    rows = proj_ref.shape[0]
    wide = ext.shape[1]

    @pl.when(pl.program_id(0) == 0)
    def _():
        ext[...] = jnp.zeros_like(ext)
        state[...] = jnp.zeros_like(state)

    ext[0:HALO, :] = ext[rows : rows + HALO, :]
    ext[HALO : HALO + rows, :] = proj_ref[:, chan : chan + wide]
    z_raw = proj_ref[:, 0:chan]
    terms = block_terms(ext, proj_ref[:, chan + wide :], conv_ref, head_ref, chan, head_width)
    _, _, conv, _, step, _, causal, log_decay, _, step_ch, log_ch, skip_ch = terms
    half = (wide - chan) // 2
    x_conv = conv[:, :chan]
    b_half = conv[:, chan : chan + half].astype(BF16)
    c_half = conv[:, chan + half :].astype(BF16)
    stepped = x_conv * step_ch
    stepped_half = stepped.astype(BF16)
    scores = dot_nt(c_half, b_half)
    log_rows = log_decay.T
    lane = iota((rows, chan), 1)
    inside = jnp.zeros((rows, chan), F32)
    for head in range(heads):
        gap = log_decay[:, head : head + 1] - log_rows[head : head + 1, :]
        mixing = (scores * jnp.exp(jnp.where(causal, gap, -1e30))).astype(BF16)
        mine = (lane >= head * head_width) & (lane < (head + 1) * head_width)
        inside = inside + dot_nn(mixing, jnp.where(mine, stepped, 0.0).astype(BF16))
    entering = state[...]
    state_ref[0] = entering
    outside = dot_nn(c_half, entering.astype(BF16)) * jnp.exp(log_ch)
    mixed = inside + outside + skip_ch * x_conv
    last = log_ch[rows - 1 : rows, :]
    tail = stepped * jnp.exp(last - log_ch)
    state[...] = entering * jnp.exp(last) + dot_tn(b_half, tail.astype(BF16))
    gated_ref[...] = mixed * (z_raw * sigmoid(z_raw))
    mixed_ref[...] = mixed
    inside_ref[...] = inside


def backward_kernel(
    heads, head_width, proj_ref, prior_ref, conv_ref, head_ref, mixed_ref, inside_ref, state_ref, grad_ref,
    slot_ref, conv_grad_ref, head_grad_ref, skip_grad_ref, ext, grad_ext, grad_state,
):
    chan = heads * head_width
    rows = proj_ref.shape[0]
    wide = ext.shape[1]
    turn = pl.program_id(0)
    first_block = turn == pl.num_programs(0) - 1

    @pl.when(turn == 0)
    def _():
        grad_ext[...] = jnp.zeros_like(grad_ext)
        grad_state[...] = jnp.zeros_like(grad_state)
        conv_grad_ref[...] = jnp.zeros_like(conv_grad_ref)
        head_grad_ref[...] = jnp.zeros_like(head_grad_ref)
        skip_grad_ref[...] = jnp.zeros_like(skip_grad_ref)

    ext[0:HALO, :] = jnp.where(first_block, 0.0, prior_ref[:, chan : chan + wide])
    ext[HALO : HALO + rows, :] = proj_ref[:, chan : chan + wide]
    terms = block_terms(ext, proj_ref[:, chan + wide :], conv_ref, head_ref, chan, head_width)
    pre, gate, conv, step_pre, step, rate, causal, log_decay, spread, step_ch, log_ch, skip_ch = terms
    half = (wide - chan) // 2
    x_conv = conv[:, :chan]
    b_half = conv[:, chan : chan + half].astype(BF16)
    c_half = conv[:, chan + half :].astype(BF16)
    stepped = x_conv * step_ch
    stepped_half = stepped.astype(BF16)
    grad_mixed = grad_ref[...]
    grad_half = grad_mixed.astype(BF16)
    inside = inside_ref[...]
    outside = mixed_ref[...] - inside - skip_ch * x_conv

    scores = dot_nt(c_half, b_half)
    log_rows = log_decay.T
    lane = iota((rows, chan), 1)
    grad_scores = jnp.zeros((rows, rows), F32)
    grad_inner = jnp.zeros((rows, chan), F32)
    for head in range(heads):
        gap = log_decay[:, head : head + 1] - log_rows[head : head + 1, :]
        decay = jnp.exp(jnp.where(causal, gap, -1e30))
        mixing = (scores * decay).astype(BF16)
        mine = (lane >= head * head_width) & (lane < (head + 1) * head_width)
        grad_mine = jnp.where(mine, grad_mixed, 0.0).astype(BF16)
        grad_scores = grad_scores + dot_nt(grad_mine, stepped_half) * decay
        grad_inner = grad_inner + dot_tn(mixing, grad_mine)
    scores_half = grad_scores.astype(BF16)

    entering = state_ref[0]
    left = grad_state[...]
    left_half = left.astype(BF16)
    grad_outer = (grad_mixed * jnp.exp(log_ch)).astype(BF16)
    last = log_ch[rows - 1 : rows, :]
    fade = jnp.exp(last - log_ch)
    tail = stepped * fade
    grad_tail = dot_nn(b_half, left_half)
    tail_term = tail * grad_tail
    grad_c = dot_nt(grad_outer, entering.astype(BF16)) + dot_nn(scores_half, b_half)
    grad_b = dot_nt(tail.astype(BF16), left_half) + dot_tn(scores_half, c_half)
    grad_last = jnp.sum(tail_term, axis=0, keepdims=True) + jnp.exp(last) * jnp.sum(
        left * entering, axis=0, keepdims=True
    )
    grad_state[...] = left * jnp.exp(last) + dot_tn(c_half, grad_outer)

    grad_stepped = grad_inner + grad_tail * fade
    log_term = (
        grad_half.astype(F32) * inside
        + grad_mixed * outside
        - stepped_half.astype(F32) * grad_inner
        - tail_term
    )
    row = iota((rows, chan), 0)
    log_term = log_term + jnp.where(row == rows - 1, grad_last, 0.0)

    def per_head(values):
        return lax.dot_general(
            values, spread, (((1,), (1,)), ((), ())), precision=PRECISE, preferred_element_type=F32
        )

    later = (iota((rows, rows), 0) <= iota((rows, rows), 1)).astype(F32)
    grad_rate_step = dot_f32(later, per_head(log_term))
    grad_step = per_head(grad_stepped * x_conv) + grad_rate_step * rate
    grad_step_raw = grad_step * sigmoid(step_pre)
    head_grad_ref[0:1, :] += jnp.sum(grad_step_raw, axis=0, keepdims=True)
    head_grad_ref[1:2, :] += jnp.sum(grad_rate_step * step, axis=0, keepdims=True) * rate
    skip_grad_ref[0:1, :] += jnp.sum(grad_mixed * x_conv, axis=0, keepdims=True)

    grad_x = grad_stepped * step_ch + grad_mixed * skip_ch
    slope = gate * (1.0 + pre * (1.0 - gate))
    grad_ext[rows : rows + HALO, :] = grad_ext[0:HALO, :]
    grad_ext[0:rows, 0:chan] = grad_x * slope[:, :chan]
    grad_ext[0:rows, chan : chan + half] = grad_b * slope[:, chan : chan + half]
    grad_ext[0:rows, chan + half :] = grad_c * slope[:, chan + half :]
    grad_pre = grad_ext[0:rows, :]
    grad_raw = jnp.zeros((rows, wide), F32)
    for tap in range(4):
        grad_raw = grad_raw + conv_ref[tap : tap + 1, :] * grad_ext[3 - tap : 3 - tap + rows, :]
        first = HALO - 3 + tap
        conv_grad_ref[tap : tap + 1, :] += jnp.sum(
            grad_pre * ext[first : first + rows, :], axis=0, keepdims=True
        )
    conv_grad_ref[4:5, :] += jnp.sum(grad_pre, axis=0, keepdims=True)
    slot_ref[:, 0:wide] = grad_raw.astype(BF16)
    slot_ref[:, wide:] = grad_step_raw.astype(BF16)


def mixer_forward(proj, conv_pack, head_pack, heads, head_width, wide):
    total, columns = proj.shape
    chan = heads * head_width
    state_width = (wide - chan) // 2
    blocks = total // BLOCK
    row_spec = pl.BlockSpec((BLOCK, chan), lambda i: (i, 0))
    rows = jax.ShapeDtypeStruct((total, chan), F32)
    return pl.pallas_call(
        functools.partial(forward_kernel, heads, head_width),
        grid=(blocks,),
        in_specs=[
            pl.BlockSpec((BLOCK, columns), lambda i: (i, 0)),
            pl.BlockSpec(conv_pack.shape, lambda i: (0, 0)),
            pl.BlockSpec(head_pack.shape, lambda i: (0, 0)),
        ],
        out_specs=[row_spec, row_spec, row_spec, pl.BlockSpec((1, state_width, chan), lambda i: (i, 0, 0))],
        out_shape=[rows, rows, rows, jax.ShapeDtypeStruct((blocks, state_width, chan), F32)],
        scratch_shapes=[pltpu.VMEM((BLOCK + HALO, wide), F32), pltpu.VMEM((state_width, chan), F32)],
        compiler_params=pltpu.CompilerParams(vmem_limit_bytes=32 << 20),
        cost_estimate=pl.CostEstimate(flops=4 * 10**9, bytes_accessed=7 << 20, transcendentals=2 << 20),
        name="mixer_forward",
    )(proj, conv_pack, head_pack)


def mixer_backward(proj, conv_pack, head_pack, mixed, inside, states, grad_mixed, heads, head_width, wide):
    total, columns = proj.shape
    chan = heads * head_width
    state_width = (wide - chan) // 2
    blocks = total // BLOCK
    ratio = BLOCK // HALO
    back = lambda i: (blocks - 1 - i, 0)
    row_spec = pl.BlockSpec((BLOCK, chan), back)
    fixed = lambda i: (0, 0)
    out_columns = wide + LANES
    return pl.pallas_call(
        functools.partial(backward_kernel, heads, head_width),
        grid=(blocks,),
        in_specs=[
            pl.BlockSpec((BLOCK, columns), back),
            pl.BlockSpec((HALO, columns), lambda i: (jnp.maximum((blocks - 1 - i) * ratio - 1, 0), 0)),
            pl.BlockSpec(conv_pack.shape, fixed),
            pl.BlockSpec(head_pack.shape, fixed),
            row_spec,
            row_spec,
            pl.BlockSpec((1, state_width, chan), lambda i: (blocks - 1 - i, 0, 0)),
            row_spec,
        ],
        out_specs=[
            pl.BlockSpec((BLOCK, out_columns), back),
            pl.BlockSpec((HALO, wide), fixed),
            pl.BlockSpec((HALO, LANES), fixed),
            pl.BlockSpec((HALO, chan), fixed),
        ],
        out_shape=[
            jax.ShapeDtypeStruct((total, out_columns), BF16),
            jax.ShapeDtypeStruct((HALO, wide), F32),
            jax.ShapeDtypeStruct((HALO, LANES), F32),
            jax.ShapeDtypeStruct((HALO, chan), F32),
        ],
        scratch_shapes=[
            pltpu.VMEM((BLOCK + HALO, wide), F32),
            pltpu.VMEM((BLOCK + HALO, wide), F32),
            pltpu.VMEM((state_width, chan), F32),
        ],
        compiler_params=pltpu.CompilerParams(vmem_limit_bytes=40 << 20),
        cost_estimate=pl.CostEstimate(flops=12 * 10**9, bytes_accessed=9 << 20, transcendentals=2 << 20),
        name="mixer_backward",
    )(proj, proj, conv_pack, head_pack, mixed, inside, states, grad_mixed)


def from_columns(block_for):
    count = lax.axis_size("col")
    got = [block_for(0)]
    for j in range(1, count):
        pairs = [((i + j) % count, i) for i in range(count)]
        got.append(lax.ppermute(block_for((count - j) % count), "col", pairs))
    return got


def scatter_sum(partial):
    rows, cols = lax.axis_size("row"), lax.axis_size("col")
    pair = 2 if rows % 2 == 0 else 1
    chips = rows // pair
    row = lax.axis_index("row")
    chip, core = row // pair, row % pair
    tokens, width = partial.shape[0] // rows, partial.shape[1] // cols
    blocks = partial.reshape(chips, pair, tokens, cols * width)
    keep = lax.dynamic_index_in_dim(blocks, core, 1, keepdims=False)
    if pair == 2:
        send = lax.dynamic_index_in_dim(blocks, 1 - core, 1, keepdims=False).astype(BF16)
        swap = [(i, i ^ 1) for i in range(rows)]
        keep = keep + lax.ppermute(send, "row", swap).astype(F32)
    total = None
    for dx in range(chips):
        mine = lax.dynamic_index_in_dim(keep, (chip + dx) % chips, 0, keepdims=False)
        for dc in range(cols):
            piece = mine[:, dc * width : (dc + 1) * width]
            if dx or dc:
                pairs = []
                for r in range(rows):
                    for c in range(cols):
                        there = ((r // pair + dx) % chips) * pair + r % pair
                        pairs.append((r * cols + c, there * cols + (c + dc) % cols))
                piece = lax.ppermute(piece.astype(BF16), ("row", "col"), pairs).astype(F32)
            total = piece if total is None else total + piece
    return total


def sum_kernel(rows, cols, own_ref, out_ref, got, send_sem, recv_sem):
    dp, row, col = lax.axis_index("dp"), lax.axis_index("row"), lax.axis_index("col")
    peers = [
        (dp, lax.rem(row + k // cols, rows), lax.rem(col + k % cols, cols)) for k in range(1, rows * cols)
    ]
    barrier = pltpu.get_barrier_semaphore()
    for peer in peers:
        pl.semaphore_signal(barrier, inc=1, device_id=peer, device_id_type=pl.DeviceIdType.MESH)
    pl.semaphore_wait(barrier, len(peers))
    copies = []
    for k, peer in enumerate(peers):
        copy = pltpu.make_async_remote_copy(
            src_ref=own_ref,
            dst_ref=got.at[k],
            send_sem=send_sem.at[k],
            recv_sem=recv_sem.at[k],
            device_id=peer,
            device_id_type=pl.DeviceIdType.MESH,
        )
        copy.start()
        copies.append(copy)
    for copy in copies:
        copy.wait()
    total = own_ref[...]
    for k in range(len(peers)):
        total = total + got[k]
    out_ref[...] = total


def sum_over_group(values):
    rows, cols = lax.axis_size("row"), lax.axis_size("col")
    others = rows * cols - 1
    return pl.pallas_call(
        functools.partial(sum_kernel, rows, cols),
        out_shape=jax.ShapeDtypeStruct(values.shape, values.dtype),
        in_specs=[pl.BlockSpec(memory_space=pltpu.VMEM)],
        out_specs=pl.BlockSpec(memory_space=pltpu.VMEM),
        scratch_shapes=[
            pltpu.VMEM((others, *values.shape), values.dtype),
            pltpu.SemaphoreType.DMA((others,)),
            pltpu.SemaphoreType.DMA((others,)),
        ],
        compiler_params=pltpu.CompilerParams(collective_id=0, has_side_effects=True),
        name="sum_over_group",
    )(values)


def dp_scatter(matrix):
    count = lax.axis_size("dp")
    index = lax.axis_index("dp")
    unit = count * 16
    rows = -(-matrix.shape[0] // unit) * unit
    blocks = pad_to(matrix, rows, matrix.shape[1]).reshape(count, rows // count, matrix.shape[1])
    total = lax.dynamic_index_in_dim(blocks, index, 0, keepdims=False).astype(F32)
    for k in range(1, count):
        send = lax.dynamic_index_in_dim(blocks, (index + k) % count, 0, keepdims=False)
        pairs = [(i, (i + k) % count) for i in range(count)]
        total = total + lax.ppermute(send, "dp", pairs).astype(F32)
    return total.astype(BF16)


def dp_gather(pieces):
    every = lax.all_gather(jnp.concatenate(pieces, axis=0), "dp", axis=0, tiled=False)
    got, at = [], 0
    for piece in pieces:
        part = every[:, at : at + piece.shape[0]]
        got.append(part.reshape(-1, piece.shape[1]))
        at += piece.shape[0]
    return got


def row_sum(matrix):
    count = lax.axis_size("row")
    if count & (count - 1):
        return lax.psum(matrix.astype(F32), "row").astype(BF16)
    bit = 1
    while bit < count:
        other = lax.ppermute(matrix, "row", [(i, i ^ bit) for i in range(count)])
        matrix = (matrix.astype(F32) + other.astype(F32)).astype(BF16)
        bit *= 2
    return matrix


def pad_to(matrix, rows, columns):
    return jnp.pad(matrix, ((0, rows - matrix.shape[0]), (0, columns - matrix.shape[1])))


def body(
    hidden,
    cotangent,
    norm_gain,
    weight_z,
    weight_x,
    weight_dt,
    weight_bc,
    conv_weight,
    conv_bias,
    bc_conv_weight,
    bc_conv_bias,
    dt_bias,
    decay_log,
    skip_gain,
    gate_gain,
    out_weight,
):
    row_count = lax.axis_size("row")
    col_count = lax.axis_size("col")
    col_index = lax.axis_index("col")
    model_width = hidden.shape[1]
    width = weight_z.shape[0]
    chan = weight_z.shape[1] // col_count
    heads = weight_dt.shape[1] // col_count
    head_width = chan // heads
    bc_width = weight_bc.shape[1]
    wide = chan + bc_width
    inner = chan * row_count * col_count

    def own_first(matrix, axis):
        return jnp.roll(matrix, -col_index * width, axis)

    def by_col(matrix, k):
        split = matrix.reshape(matrix.shape[0], col_count, matrix.shape[1] // col_count)
        return lax.dynamic_index_in_dim(split, (col_index + k) % col_count, 1, keepdims=False)

    def weights_for(k):
        return jnp.concatenate(
            [by_col(weight_z, k), by_col(weight_x, k), weight_bc, by_col(weight_dt, k)], axis=1
        )

    weights = jnp.concatenate(from_columns(weights_for), axis=0)
    weights = jnp.pad(weights, ((0, 0), (0, LANES - heads)))
    weights, cot_later, out_weight = lax.optimization_barrier((weights, cotangent, out_weight))

    def out_rows_for(k):
        split = out_weight.reshape(col_count, chan, out_weight.shape[1])
        return lax.dynamic_index_in_dim(split, (col_index + k) % col_count, 0, keepdims=False)

    out_own = jnp.concatenate(from_columns(out_rows_for), axis=1)
    cot_half = cot_later.astype(BF16)
    cot_wide = jnp.concatenate(from_columns(lambda k: cot_half), axis=1)

    inv_rms = lax.rsqrt(jnp.mean(hidden * hidden, axis=1, keepdims=True) + EPSILON)
    scaled = (own_first(hidden, 1) * inv_rms * own_first(norm_gain, 0)[None, :]).astype(BF16)
    gathered = lax.all_gather(scaled, "row", axis=0, tiled=True)
    cot_rows = lax.all_gather(cot_wide, "row", axis=0, tiled=True)
    proj = jnp.dot(gathered, weights, preferred_element_type=F32)

    conv_pack = pad_to(
        jnp.concatenate(
            [
                jnp.concatenate([conv_weight, bc_conv_weight], axis=1),
                jnp.concatenate([conv_bias, bc_conv_bias])[None, :],
            ],
            axis=0,
        ),
        HALO,
        wide,
    )
    head_pack = pad_to(jnp.stack([dt_bias, decay_log, skip_gain]), HALO, LANES)
    gated, mixed, inside, states = mixer_forward(proj, conv_pack, head_pack, heads, head_width, wide)

    grad_gate_out = dot_nt(cot_rows, out_own)
    grad_hat = grad_gate_out * gate_gain[None, :]
    sums = sum_over_group(
        jnp.stack([jnp.sum(gated * gated, axis=1), jnp.sum(grad_hat * gated, axis=1)])
    )
    inv_gate = lax.rsqrt(sums[0] / inner + EPSILON)[:, None]
    gate_dot = sums[1][:, None] * inv_gate
    gate_hat = gated * inv_gate
    grad_gated = inv_gate * (grad_hat - gate_hat * (gate_dot / inner))
    z_raw = proj[:, :chan]
    z_gate = sigmoid(z_raw)
    grad_mixed = grad_gated * (z_raw * z_gate)
    grad_z = (grad_gated * mixed * (z_gate * (1.0 + z_raw * (1.0 - z_gate)))).astype(BF16)
    gate_out = (gate_hat * gate_gain[None, :]).astype(BF16)
    grad_gate_gain = jnp.sum(grad_gate_out * gate_hat, axis=0)

    out_part = dot_tn(gate_out, cot_rows)
    z_part = dot_tn(gathered, grad_z)
    grad_mixed, out_part, z_part = lax.optimization_barrier((grad_mixed, out_part, z_part))
    slots, conv_grads, head_grads, skip_grads = mixer_backward(
        proj, conv_pack, head_pack, mixed, inside, states, grad_mixed, heads, head_width, wide
    )

    def to_col_blocks(matrix):
        return matrix.reshape(col_count, matrix.shape[0] // col_count, matrix.shape[1])

    def in_col_order(relative, axis):
        return jnp.roll(relative, col_index, axis)

    out_rel = from_columns(lambda k: out_part[:, k * width : (k + 1) * width].astype(BF16))
    z_blocks = to_col_blocks(z_part)
    z_rel = from_columns(lambda k: z_blocks[k].astype(BF16))
    (early,) = dp_gather(
        [dp_scatter(jnp.concatenate([piece.reshape(-1, chan) for piece in out_rel + z_rel], axis=0))]
    )
    out_size = chan * width // chan
    out_sum = early[: out_size * col_count].reshape(col_count, chan, width)
    z_sum = early[out_size * col_count :].reshape(col_count, width, chan)
    grad_out_weight = in_col_order(out_sum, 0).reshape(col_count * chan, width).astype(F32)
    grad_weight_z = (
        in_col_order(z_sum, 0).transpose(1, 0, 2).reshape(width, col_count * chan).astype(F32)
    )

    branch_out = scatter_sum(dot_nn(gate_out, out_own))
    hidden_col = lax.dynamic_slice_in_dim(hidden, col_index * width, width, 1)
    output = hidden_col + branch_out

    grad_slots = jnp.concatenate([grad_z, slots], axis=1)
    grad_scaled = scatter_sum(dot_nt(grad_slots, weights))

    late_part = dot_tn(gathered, slots)
    gain_part = jnp.sum(z_part * weights[:, :chan].astype(F32), axis=1) + jnp.sum(
        late_part * weights[:, chan:].astype(F32), axis=1
    )
    late_blocks = to_col_blocks(late_part[:, : wide + heads])
    gain_blocks = gain_part.reshape(col_count, 1, width)
    bc_rows = conv_grads[:5, chan:]

    def late_for(k):
        return late_blocks[k].astype(BF16)

    def small_for(k):
        return jnp.concatenate([pad_to(bc_rows, 5, width), gain_blocks[k]], axis=0)

    late_rel = from_columns(late_for)
    small_rel = from_columns(small_for)
    x_rows = [piece[:, :chan] for piece in late_rel]
    dt_rows = [piece[:, wide:].reshape(-1, chan) for piece in late_rel]
    skip_sum = jnp.sum(skip_grads[0].reshape(heads, head_width), axis=1)
    head_row = jnp.concatenate([head_grads[0, :heads], head_grads[1, :heads], skip_sum])[None, :]
    dp_rows = x_rows + dt_rows + [
        conv_grads[:5, :chan].astype(BF16),
        grad_gate_gain[None, :].astype(BF16),
        pad_to(head_row, 1, chan).astype(BF16),
    ]
    x_piece = dp_scatter(jnp.concatenate(dp_rows, axis=0))
    bc_mine = sum(piece[:, chan:wide].astype(F32) for piece in late_rel).astype(BF16)
    small_mine = sum(small_rel).astype(BF16)
    shared_rows = jnp.concatenate(
        [bc_mine, small_mine[:5, :bc_width], small_mine[5].reshape(-1, bc_width)], axis=0
    )
    bc_piece = dp_scatter(row_sum(shared_rows))
    late, shared = dp_gather([x_piece, bc_piece])
    shared = shared.astype(F32)

    dt_count = width * heads // chan
    x_sum = late[: width * col_count].reshape(col_count, width, chan)
    grad_weight_x = (
        in_col_order(x_sum, 0).transpose(1, 0, 2).reshape(width, col_count * chan).astype(F32)
    )
    at = width * col_count
    dt_sum = late[at : at + dt_count * col_count].reshape(col_count, width, heads)
    grad_weight_dt = (
        in_col_order(dt_sum, 0).transpose(1, 0, 2).reshape(width, col_count * heads).astype(F32)
    )
    rest = late[at + dt_count * col_count :].astype(F32)
    grad_weight_bc = shared[:width]
    gain_col = lax.dynamic_slice_in_dim(norm_gain, col_index * width, width, 0)
    grad_norm_gain = shared[width + 5 : width + 5 + width // bc_width].reshape(-1) / gain_col

    normed_col = hidden_col * inv_rms
    grad_in = grad_scaled * gain_col[None, :]
    input_dot = sum(from_columns(lambda k: jnp.sum(grad_in * normed_col, axis=1)))
    grad_hidden = cotangent + inv_rms * (grad_in - normed_col * (input_dot[:, None] / model_width))
    return (
        output,
        grad_hidden,
        grad_norm_gain,
        grad_weight_z,
        grad_weight_x,
        grad_weight_dt,
        grad_weight_bc,
        rest[0:4],
        rest[4],
        shared[width : width + 4],
        shared[width + 4],
        rest[6, :heads],
        rest[6, heads : 2 * heads],
        rest[6, 2 * heads : 3 * heads],
        rest[5],
        grad_out_weight,
    )


def solution(mesh):
    in_specs = (
        P(("dp", "row"), None),
        P(("dp", "row"), "col"),
        P(),
        P("col", "row"),
        P("col", "row"),
        P("col", "row"),
        P("col", None),
        P(None, ("row", "col")),
        P(("row", "col")),
        P(),
        P(),
        P(("row", "col")),
        P(("row", "col")),
        P(("row", "col")),
        P(("row", "col")),
        P("row", "col"),
    )
    out_specs = (
        P(("dp", "row"), "col"),
        P(("dp", "row"), "col"),
        P("col"),
        P("col", "row"),
        P("col", "row"),
        P("col", "row"),
        P("col", None),
        P(None, ("row", "col")),
        P(("row", "col")),
        P(),
        P(),
        P(("row", "col")),
        P(("row", "col")),
        P(("row", "col")),
        P(("row", "col")),
        P("row", "col"),
    )
    return jax.shard_map(body, mesh=mesh, in_specs=in_specs, out_specs=out_specs, check_vma=False)
```
